32 devices in a mesh: cache: 8 (over z, x), owner: 4 (over y, core).
Axes of the slice: x: 2, y: 2, z: 4, core: 2. Of those that a mesh axis runs over, the one named last changes fastest.
Arguments:
- cache: bfloat16 [32, 4, 128, 256], P('cache'), may hold values from -2.5 to 2.5
- backing: bfloat16 [32, 32, 128, 256], P('cache', 'owner'), may hold values from -2.5 to 2.5
- resident: int32 [32, 4], P('cache'), may hold values from 0 to 31, as said below
- promote: int32 [32, 2], P('cache'), may hold values from 0 to 31, as said below
- victim: int32 [32, 2], P('cache'), may hold values from 0 to 3, as said below
- lookups: int32 [2, 4096, 32, 8], P(None, 'owner', 'cache'), may hold values from 0 to 511
- route: int32 [2, 4, 1024], P(None, 'owner'), may hold values from 0 to 1023, each once within a row
- dcn_down: bfloat16 [8192, 128], P('cache'), may hold values from -0.0625 to 0.0625
- dcn_up: bfloat16 [128, 8192], P(None, 'cache'), may hold values from -0.5 to 0.5
- dcn_bias: float32 [8192], replicated, may hold values from -5 to 5
- mlp_in: bfloat16 [8192, 1024], P('cache'), may hold values from -0.0625 to 0.0625
- mlp_bias: float32 [1024], replicated, may hold values from -3 to 3
- mlp_out: float32 [1024], replicated, may hold values from -0.1875 to 0.1875
- out_bias: float32 [1], replicated, may hold values from -4 to 4
Outputs:
- scores: float32 [2, 4, 1024], P(None, 'owner', 'cache')
- new_cache: bfloat16 [32, 4, 128, 256], P('cache')
- new_backing: bfloat16 [32, 32, 128, 256], P('cache', 'owner')
The draws below stay inside these ranges and needn't reach their ends.
Inputs may be any that keep to these rules, and one draw needn't show every extreme that they name: `resident`: for each feature, 4 distinct backing blocks. `promote`: for each feature, 2 distinct backing blocks, none of them in that feature's resident; block k belongs to owner k // 8. `victim`: for each feature, 2 distinct slots. `route`: each batch and owner group holds every request index once.
All inputs are finite; a program needn't handle non-finite values.
Results may differ from the reference program's by a relative error of at most 0.004.
Values may be sent and summed in bfloat16 or wider, within the bound.
A program may use at most 128 MiB of HBM per device.

```python
import math
import jax
import jax.numpy as jnp
import numpy as np
from jax import lax

E = 256
F = 32
HID = 1024
RANK = 128
BLOCK = 128
BAG = 8
BATCHES = 2
SLOTS = 4
OWN_BLK = 8
PROM = 2
D0 = 8192
BACK = 32
REQ_G = 1024
REQ = 4096
N_OWNER = 4


def common_plan(key):
    base_key = jax.random.fold_in(key, 11)

    def single(feature):
        feature_key = jax.random.fold_in(base_key, feature)
        first_key, second_key, third_key = jax.random.split(feature_key, 3)
        owners = BACK // OWN_BLK
        hot_owner = jax.random.randint(first_key, (), 0, owners)
        order_rank = jax.random.permutation(second_key, BACK).astype(jnp.int32)
        block_numbers = jnp.arange(BACK, dtype=jnp.int32)
        leaning = (feature % 2 == 0) & (block_numbers // OWN_BLK == hot_owner)
        promote_score = order_rank - jnp.where(leaning, BACK, 0)
        promoted = jnp.argsort(promote_score, stable=True)[:PROM].astype(jnp.int32)
        chosen_set = jnp.any(block_numbers[:, None] == promoted[None, :], axis=1)
        resident = jnp.argsort(order_rank + jnp.where(chosen_set, 2 * BACK, 0), stable=True)[:SLOTS].astype(jnp.int32)
        victims = jax.random.permutation(third_key, SLOTS)[:PROM].astype(jnp.int32)
        return (resident, promoted, victims)
    return jax.vmap(single)(jnp.arange(F, dtype=jnp.int32))


def draw_resident(key, part):
    return common_plan(key)[0]


def draw_promote(key, part):
    return common_plan(key)[1]


def draw_victim(key, part):
    return common_plan(key)[2]


def place_ends(entries, own_key, low, high):
    dims = entries.shape
    place = [jax.random.randint(jax.random.fold_in(own_key, axis), (), 0, dims[axis]) for axis in range(len(dims))]
    entries = entries.at[tuple(place)].set(low)
    longest = dims.index(max(dims))
    place[longest] = (place[longest] + 1) % dims[longest]
    return entries.at[tuple(place)].set(high)


def levels(rng, extent, shards, low, largest):
    def one(position, parts):
        draws = jax.random.uniform(jax.random.fold_in(jax.random.fold_in(rng, 6), position), (parts,), jnp.float32, low / len(shards), largest / len(shards))
        return jnp.repeat(jnp.exp(draws), extent[position] // parts).reshape((-1,) + (1,) * (len(extent) - position - 1))

    gain = one(*shards[0])
    for cut in shards[1:]:
        gain = gain * one(*cut)
    return gain


def rank_bounds(count, lean):
    portions = [(1 << 20) // math.isqrt(rank ** lean) + 1 for rank in range(1, count + 1)]
    scale = 1 + sum(portions) // (1 << 30)
    return np.cumsum(np.array([max(1, weight // scale) for weight in portions]))


def ranked_ids(rng, shape, amount, slope):
    grid = rank_bounds(amount, slope)
    lot = jax.random.randint(jax.random.fold_in(rng, 1), shape, 0, int(grid[amount - 1]))
    grade = jnp.searchsorted(jnp.asarray(grid, jnp.int32), lot, side="right")
    return jax.random.permutation(jax.random.fold_in(rng, 2), amount)[grade].astype(jnp.int32)


def scatter_about(own_key, shape, width, most, cuts=(), kind=jnp.bfloat16):
    array = width * jax.random.normal(own_key, shape, jnp.float32)
    if cuts:
        array = array * levels(own_key, shape, cuts, -0.22, 0.18)
    return jnp.clip(array, -most, most).astype(kind)


def setup_inputs(seed: int = 0) -> dict:
    key_of = jax.random.split(jax.random.key(seed), 15)
    cache = scatter_about(key_of[0], (F, SLOTS, BLOCK, E), 0.35, 2.5, ((0, 8),))
    backing = scatter_about(key_of[1], (F, BACK, BLOCK, E), 0.35, 2.5, ((0, 8), (1, 4)))
    resident = draw_resident(jax.random.fold_in(key_of[14], 71), 0)
    promote = draw_promote(jax.random.fold_in(key_of[14], 71), 0)
    victim = draw_victim(jax.random.fold_in(key_of[14], 71), 0)
    lookups = place_ends(ranked_ids(key_of[5], (BATCHES, REQ, F, BAG), SLOTS * BLOCK, 2), jax.random.fold_in(key_of[5], 3), 0, (SLOTS * BLOCK) - 1).astype(jnp.int32)
    route = jax.vmap(lambda own: jax.random.permutation(own, REQ_G))(jax.random.split(key_of[6], BATCHES * N_OWNER)).reshape((BATCHES, N_OWNER, REQ_G)).astype(jnp.int32)
    dcn_down = scatter_about(key_of[7], (D0, RANK), D0 ** -0.5, 0.0625, ((0, 8),))
    dcn_up = scatter_about(key_of[8], (RANK, D0), RANK ** -0.5, 0.5, ((1, 8),))
    dcn_bias = scatter_about(key_of[9], (D0,), 1.0, 5.0, (), jnp.float32)
    mlp_in = scatter_about(key_of[10], (D0, HID), D0 ** -0.5, 0.0625, ((0, 8),))
    mlp_bias = scatter_about(key_of[11], (HID,), 0.5, 3.0, (), jnp.float32)
    mlp_out = scatter_about(key_of[12], (HID,), HID ** -0.5, 0.1875, (), jnp.float32)
    out_bias = scatter_about(key_of[13], (1,), 1.0, 4.0, (), jnp.float32)
    return dict(cache=cache, backing=backing, resident=resident, promote=promote, victim=victim, lookups=lookups, route=route, dcn_down=dcn_down, dcn_up=dcn_up, dcn_bias=dcn_bias, mlp_in=mlp_in, mlp_bias=mlp_bias, mlp_out=mlp_out, out_bias=out_bias)


def take_rows(table, wanted):
    return jax.vmap(lambda rows, chosen: rows[chosen])(table, wanted)


def dense_rows(features, dcn_down, dcn_up, dcn_bias, mlp_in, mlp_bias, mlp_out, out_bias):
    low = jnp.dot(features, dcn_down, preferred_element_type=jnp.float32).astype(jnp.bfloat16)
    gate = jnp.dot(low, dcn_up, preferred_element_type=jnp.float32) + dcn_bias
    crossed = (features * gate + features).astype(jnp.bfloat16)
    hidden = jnp.maximum(jnp.dot(crossed, mlp_in, preferred_element_type=jnp.float32) + mlp_bias, 0.0)
    return jnp.sum(hidden * mlp_out, axis=-1) + out_bias[0]


def reference(cache, backing, resident, promote, victim, lookups, route, dcn_down, dcn_up, dcn_bias, mlp_in, mlp_bias, mlp_out, out_bias):
    fetched = take_rows(backing, promote)
    evicted = take_rows(cache, victim)
    leaving = take_rows(resident, victim)
    slot_numbers = jnp.arange(SLOTS, dtype=jnp.int32)
    block_numbers = jnp.arange(BACK, dtype=jnp.int32)
    new_cache = cache
    new_backing = backing
    for column in range(PROM):
        slot_hit = victim[:, column][:, None] == slot_numbers[None, :]
        new_cache = jnp.where(slot_hit[:, :, None, None], fetched[:, column][:, None], new_cache)
        block_hit = leaving[:, column][:, None] == block_numbers[None, :]
        new_backing = jnp.where(block_hit[:, :, None, None], evicted[:, column][:, None], new_backing)
    table = new_cache.reshape(F, SLOTS * BLOCK, E)

    def pool_feature(pair):
        rows, wanted = pair
        return jnp.sum(rows[wanted].astype(jnp.float32), axis=1).astype(jnp.bfloat16)

    step = min(1024, REQ)
    results = []
    for batch_turn in range(BATCHES):
        pooled = lax.map(pool_feature, (table, jnp.transpose(lookups[batch_turn], (1, 0, 2))))
        pooled = jnp.transpose(pooled, (1, 0, 2))
        offsets = (jnp.arange(N_OWNER, dtype=jnp.int32) * REQ_G)[:, None]
        order = (route[batch_turn] + offsets).reshape(-1)
        features = pooled[order].reshape(REQ // step, step, D0)
        scored = lax.map(lambda block_rows: dense_rows(block_rows, dcn_down, dcn_up, dcn_bias, mlp_in, mlp_bias, mlp_out, out_bias), features)
        results.append(scored.reshape(N_OWNER, REQ_G))
    scores = jnp.stack(results)
    return scores, new_cache, new_backing
```

```python
import jax
import jax.numpy as jnp
from jax import lax
from jax.experimental import pallas as pl
from jax.experimental.pallas import tpu as pltpu
from jax.sharding import PartitionSpec as P


def take_rows(table, wanted):
    return jax.vmap(lambda rows, chosen: rows[chosen])(table, wanted)


def promote_blocks(cache, backing, resident, promote, victim):
    held, slots, block, width = cache.shape
    own_blocks = backing.shape[1]
    promoted_count = promote.shape[1]
    owner_here = lax.axis_index("owner")
    local_index = promote - owner_here * own_blocks
    owned_here = (local_index >= 0) & (local_index < own_blocks)
    clamped = jnp.clip(local_index, 0, own_blocks - 1)
    fetched = take_rows(backing, clamped)
    outgoing = jnp.where(owned_here[:, :, None, None], fetched, jnp.zeros_like(fetched))
    arrived = lax.all_gather(outgoing, "owner", axis=0, tiled=True)
    owners = arrived.shape[0] // held
    arrived = arrived.reshape(owners, held, promoted_count, block, width)
    source = promote // own_blocks
    picked = source[None] == jnp.arange(owners, dtype=jnp.int32)[:, None, None]
    promoted = jnp.sum(jnp.where(picked[..., None, None], arrived, jnp.zeros_like(arrived)), axis=0)
    evicted = take_rows(cache, victim)
    leaving = take_rows(resident, victim) - owner_here * own_blocks
    slot_numbers = jnp.arange(slots, dtype=jnp.int32)
    block_numbers = jnp.arange(own_blocks, dtype=jnp.int32)
    new_cache = cache
    new_backing = backing
    for column in range(promoted_count):
        slot_hit = victim[:, column][:, None] == slot_numbers[None, :]
        new_cache = jnp.where(slot_hit[:, :, None, None], promoted[:, column][:, None], new_cache)
        block_hit = leaving[:, column][:, None] == block_numbers[None, :]
        new_backing = jnp.where(
            block_hit[:, :, None, None], evicted[:, column][:, None], new_backing
        )
    return new_cache, new_backing


def routed(lookups, route):
    batches, count, held, bag = lookups.shape
    flat = lookups.reshape(batches, count, held * bag)
    halves = jnp.concatenate([flat // 256, flat % 256], axis=-1).astype(jnp.bfloat16)
    pick = (route[:, 0, :, None] == jnp.arange(count, dtype=jnp.int32)).astype(jnp.bfloat16)
    got = jnp.einsum("bpr,brj->bpj", pick, halves, preferred_element_type=jnp.float32)
    upper, lower = jnp.split(got, 2, axis=-1)
    return (upper * 256.0 + lower).reshape(batches * count, held * bag)


def pool_kernel(held, bag, codes_ref, table_ref, out_ref):
    rows_total, width = table_ref.shape[1], table_ref.shape[2]
    step = codes_ref.shape[0]
    lane = lax.broadcasted_iota(jnp.int32, (step, 128), 1).astype(jnp.float32)
    low_lane = lane.astype(jnp.bfloat16)
    high_lane = (lane + 128.0).astype(jnp.bfloat16)
    one = jnp.ones((step, 128), jnp.bfloat16)
    zero = jnp.zeros((step, 128), jnp.bfloat16)
    for f in range(held):
        parts = [zero] * (rows_total // 128)
        for l in range(bag):
            j = f * bag + l
            spread = jnp.broadcast_to(codes_ref[:, j : j + 1], (step, 128))
            for base in range(0, rows_total, 256):
                near = (spread - float(base)).astype(jnp.bfloat16)
                for half, numbers in enumerate((low_lane, high_lane)):
                    s = base // 128 + half
                    if s < len(parts):
                        parts[s] = parts[s] + jnp.where(near == numbers, one, zero)
        counts = jnp.concatenate(parts, axis=1)
        out_ref[:, f * width : (f + 1) * width] = jnp.dot(
            counts, table_ref[f], preferred_element_type=jnp.float32
        ).astype(jnp.bfloat16)


def pool(codes, table, bag):
    count = codes.shape[0]
    held, rows_total, width = table.shape
    step = min(256, count)
    return pl.pallas_call(
        lambda c, t, o: pool_kernel(held, bag, c, t, o),
        grid=(count // step,),
        in_specs=[
            pl.BlockSpec((step, held * bag), lambda i: (i, 0)),
            pl.BlockSpec((held, rows_total, width), lambda i: (0, 0, 0)),
        ],
        out_specs=pl.BlockSpec((step, held * width), lambda i: (i, 0)),
        out_shape=jax.ShapeDtypeStruct((count, held * width), jnp.bfloat16),
        cost_estimate=pl.CostEstimate(
            flops=2 * count * held * rows_total * width, bytes_accessed=count * held * width * 2, transcendentals=0
        ),
    )(codes, table)


def on_device(
    cache,
    backing,
    resident,
    promote,
    victim,
    lookups,
    route,
    dcn_down,
    dcn_up,
    dcn_bias,
    mlp_in,
    mlp_bias,
    mlp_out,
    out_bias,
):
    held, slots, block, width = cache.shape
    new_cache, new_backing = promote_blocks(cache, backing, resident, promote, victim)
    codes = routed(lookups, route)
    table = new_cache.reshape(held, slots * block, width)
    x0 = pool(codes, table, lookups.shape[3])
    batches, group = lookups.shape[0], lookups.shape[1]
    here = lax.axis_index("cache")
    devices = lax.axis_size("cache")
    low = lax.psum(jnp.dot(x0, dcn_down, preferred_element_type=jnp.float32), "cache").astype(jnp.bfloat16)
    own_dims = x0.shape[1]
    bias = lax.dynamic_slice_in_dim(dcn_bias, here * own_dims, own_dims, 0)
    gate = jnp.dot(low, dcn_up, preferred_element_type=jnp.float32) + bias
    x1 = (x0 * gate + x0).astype(jnp.bfloat16)
    partial = jnp.dot(x1, mlp_in, preferred_element_type=jnp.float32).astype(jnp.bfloat16)
    per = group // devices
    partial = partial.reshape(batches, devices, per, -1).transpose(1, 0, 2, 3).reshape(devices * batches * per, -1)
    before = lax.psum_scatter(partial, "cache", scatter_dimension=0, tiled=True).astype(jnp.float32)
    hidden = jnp.maximum(before + mlp_bias, 0.0)
    scores = jnp.sum(hidden * mlp_out, axis=-1) + out_bias[0]
    return (scores.reshape(batches, 1, per), new_cache, new_backing)


def solution(mesh):
    in_specs = (
        P("cache", None, None, None),
        P("cache", "owner", None, None),
        P("cache", None),
        P("cache", None),
        P("cache", None),
        P(None, "owner", "cache", None),
        P(None, "owner", None),
        P("cache", None),
        P(None, "cache"),
        P(),
        P("cache", None),
        P(),
        P(),
        P(),
    )
    out_specs = (
        P(None, "owner", "cache"),
        P("cache", None, None, None),
        P("cache", "owner", None, None),
    )
    return jax.shard_map(
        on_device, mesh=mesh, in_specs=in_specs, out_specs=out_specs, check_vma=False
    )
```

```python
import jax
import jax.numpy as jnp
from jax import lax
from jax.experimental import pallas as pl
from jax.experimental.pallas import tpu as pltpu
from jax.sharding import PartitionSpec as P


def take_rows(table, wanted):
    return jax.vmap(lambda rows, chosen: rows[chosen])(table, wanted)


def promote_blocks(cache, backing, resident, promote, victim):
    held, slots, block, width = cache.shape
    own_blocks = backing.shape[1]
    promoted_count = promote.shape[1]
    owner_here = lax.axis_index("owner")
    local_index = promote - owner_here * own_blocks
    owned_here = (local_index >= 0) & (local_index < own_blocks)
    clamped = jnp.clip(local_index, 0, own_blocks - 1)
    fetched = take_rows(backing, clamped)
    outgoing = jnp.where(owned_here[:, :, None, None], fetched, jnp.zeros_like(fetched))
    arrived = lax.all_gather(outgoing, "owner", axis=0, tiled=True)
    owners = arrived.shape[0] // held
    arrived = arrived.reshape(owners, held, promoted_count, block, width)
    source = promote // own_blocks
    picked = source[None] == jnp.arange(owners, dtype=jnp.int32)[:, None, None]
    promoted = jnp.sum(jnp.where(picked[..., None, None], arrived, jnp.zeros_like(arrived)), axis=0)
    evicted = take_rows(cache, victim)
    leaving = take_rows(resident, victim) - owner_here * own_blocks
    slot_numbers = jnp.arange(slots, dtype=jnp.int32)
    block_numbers = jnp.arange(own_blocks, dtype=jnp.int32)
    new_cache = cache
    new_backing = backing
    for column in range(promoted_count):
        slot_hit = victim[:, column][:, None] == slot_numbers[None, :]
        new_cache = jnp.where(slot_hit[:, :, None, None], promoted[:, column][:, None], new_cache)
        block_hit = leaving[:, column][:, None] == block_numbers[None, :]
        new_backing = jnp.where(
            block_hit[:, :, None, None], evicted[:, column][:, None], new_backing
        )
    return new_cache, new_backing


def routed(lookups, route, devices):
    batches, count, held, bag = lookups.shape
    flat = lookups.reshape(batches, count, held * bag)
    halves = jnp.concatenate([flat // 256, flat % 256], axis=-1).astype(jnp.bfloat16)
    pick = (route[:, 0, :, None] == jnp.arange(count, dtype=jnp.int32)).astype(jnp.bfloat16)
    got = jnp.einsum("bpr,brj->bpj", pick, halves, preferred_element_type=jnp.float32)
    upper, lower = jnp.split(got, 2, axis=-1)
    codes = (upper * 256.0 + lower).reshape(batches, devices, count // devices, held * bag)
    return codes.transpose(1, 0, 2, 3).reshape(batches * count, held * bag)


def pool_kernel(held, bag, codes_ref, table_ref, out_ref):
    rows_total, width = table_ref.shape[1], table_ref.shape[2]
    step = codes_ref.shape[0]
    lane = lax.broadcasted_iota(jnp.int32, (step, 128), 1).astype(jnp.float32)
    low_lane = lane.astype(jnp.bfloat16)
    high_lane = (lane + 128.0).astype(jnp.bfloat16)
    one = jnp.ones((step, 128), jnp.bfloat16)
    zero = jnp.zeros((step, 128), jnp.bfloat16)
    for f in range(held):
        parts = [zero] * (rows_total // 128)
        for l in range(bag):
            j = f * bag + l
            spread = jnp.broadcast_to(codes_ref[:, j : j + 1], (step, 128))
            for base in range(0, rows_total, 256):
                near = (spread - float(base)).astype(jnp.bfloat16)
                for half, numbers in enumerate((low_lane, high_lane)):
                    s = base // 128 + half
                    if s < len(parts):
                        parts[s] = parts[s] + jnp.where(near == numbers, one, zero)
        counts = jnp.concatenate(parts, axis=1)
        out_ref[:, f * width : (f + 1) * width] = jnp.dot(
            counts, table_ref[f], preferred_element_type=jnp.float32
        ).astype(jnp.bfloat16)


def pool(codes, table, bag):
    count = codes.shape[0]
    held, rows_total, width = table.shape
    step = min(256, count)
    return pl.pallas_call(
        lambda c, t, o: pool_kernel(held, bag, c, t, o),
        grid=(count // step,),
        in_specs=[
            pl.BlockSpec((step, held * bag), lambda i: (i, 0)),
            pl.BlockSpec((held, rows_total, width), lambda i: (0, 0, 0)),
        ],
        out_specs=pl.BlockSpec((step, held * width), lambda i: (i, 0)),
        out_shape=jax.ShapeDtypeStruct((count, held * width), jnp.bfloat16),
        cost_estimate=pl.CostEstimate(
            flops=2 * count * held * rows_total * width, bytes_accessed=count * held * width * 2, transcendentals=0
        ),
    )(codes, table)


def dense_kernel(
    n,
    x0_ref,
    down_ref,
    up_ref,
    bias_ref,
    w_ref,
    mlp_bias_ref,
    mlp_out_ref,
    out_bias_ref,
    scores_ref,
    low_send,
    low_recv,
    low_full,
    near_send,
    near_recv,
    far_send,
    far_recv,
    total_ref,
    low_sems,
    full_sems,
    near_sems,
    far_sems,
):
    rows = x0_ref.shape[0] // n
    pair = 2 if n % 2 == 0 else 1
    lines = n // pair
    me = lax.axis_index("cache")
    line, side = me // pair, me % pair

    def at(c):
        return pl.ds(pl.multiple_of(c * rows, rows), rows)

    def send(src, dst, sems, k, c):
        copy = pltpu.make_async_remote_copy(
            src_ref=src,
            dst_ref=dst,
            send_sem=sems.at[0, k],
            recv_sem=sems.at[1, k],
            device_id={"cache": c},
            device_id_type=pl.DeviceIdType.MESH,
        )
        copy.start()
        return copy

    def dense(c):
        x0 = x0_ref[at(c), :]
        gate = jnp.dot(low_full[c], up_ref[...], preferred_element_type=jnp.float32) + bias_ref[...]
        wide = x0.astype(jnp.float32)
        x1 = (wide * gate + wide).astype(jnp.bfloat16)
        return jnp.dot(x1, w_ref[...], preferred_element_type=jnp.float32)

    barrier = pltpu.get_barrier_semaphore()
    for o in range(1, n):
        pl.semaphore_signal(
            barrier, inc=1, device_id={"cache": lax.rem(me + o, n)}, device_id_type=pl.DeviceIdType.MESH
        )
    pl.semaphore_wait(barrier, n - 1)

    copies = []
    for o in range(1, n):
        c = lax.rem(me + o, n)
        low_send[o - 1] = jnp.dot(
            x0_ref[at(c), :], down_ref[...], preferred_element_type=jnp.float32
        ).astype(jnp.bfloat16)
        copies.append(send(low_send.at[o - 1], low_recv.at[o - 1], low_sems, o - 1, c))
    low = jnp.dot(x0_ref[at(me), :], down_ref[...], preferred_element_type=jnp.float32)
    for o in range(1, n):
        copies[o - 1].wait_recv()
        low = low + low_recv[o - 1].astype(jnp.float32)
    low_full[me] = low.astype(jnp.bfloat16)
    shares = [
        send(low_full.at[me], low_full.at[me], full_sems, o - 1, lax.rem(me + o, n)) for o in range(1, n)
    ]
    for copy in shares:
        copy.wait_recv()

    offsets = list(range(1, lines)) + [0]
    nears, fars = [], []

    def first(k):
        c = lax.rem(line + offsets[k], lines) * pair + (pair - 1 - side)
        near_send[k] = dense(c).astype(jnp.bfloat16)
        nears.append(send(near_send.at[k], near_recv.at[k], near_sems, k, line * pair + (pair - 1 - side)))

    def second(k):
        c = lax.rem(line + offsets[k], lines) * pair + side
        part = dense(c)
        if pair > 1:
            nears[k].wait_recv()
            part = part + near_recv[k].astype(jnp.float32)
        if offsets[k]:
            far_send[k] = part.astype(jnp.bfloat16)
            fars.append(send(far_send.at[k], far_recv.at[k], far_sems, k, c))
        else:
            total_ref[...] = part

    for k in range(lines + 1):
        if k < lines and pair > 1:
            first(k)
        if k:
            second(k - 1)
    total = total_ref[...]
    for k, copy in enumerate(fars):
        copy.wait_recv()
        total = total + far_recv[k].astype(jnp.float32)
    hidden = jnp.maximum(total + mlp_bias_ref[...], 0.0)
    scores_ref[...] = jnp.sum(hidden * mlp_out_ref[...], axis=1, keepdims=True) + out_bias_ref[...]
    for copy in copies + shares + nears + fars:
        copy.wait_send()


def dense_stack(x0, down, up, bias, w, mlp_bias, mlp_out, out_bias):
    n = lax.axis_size("cache")
    rows = x0.shape[0] // n
    rank, hid = down.shape[1], w.shape[1]
    lines = n // 2 if n % 2 == 0 else n
    fars = max(lines - 1, 1)
    vmem = pl.BlockSpec(memory_space=pltpu.VMEM)
    return pl.pallas_call(
        lambda *refs: dense_kernel(n, *refs),
        in_specs=[vmem] * 8,
        out_specs=vmem,
        out_shape=jax.ShapeDtypeStruct((rows, 1), jnp.float32),
        scratch_shapes=[
            pltpu.VMEM((n - 1, rows, rank), jnp.bfloat16),
            pltpu.VMEM((n - 1, rows, rank), jnp.bfloat16),
            pltpu.VMEM((n, rows, rank), jnp.bfloat16),
            pltpu.VMEM((lines, rows, hid), jnp.bfloat16),
            pltpu.VMEM((lines, rows, hid), jnp.bfloat16),
            pltpu.VMEM((fars, rows, hid), jnp.bfloat16),
            pltpu.VMEM((fars, rows, hid), jnp.bfloat16),
            pltpu.VMEM((rows, hid), jnp.float32),
            pltpu.SemaphoreType.DMA((2, n - 1)),
            pltpu.SemaphoreType.DMA((2, n - 1)),
            pltpu.SemaphoreType.DMA((2, lines)),
            pltpu.SemaphoreType.DMA((2, fars)),
        ],
        compiler_params=pltpu.CompilerParams(
            collective_id=0, has_side_effects=True, vmem_limit_bytes=60 * 1024 * 1024
        ),
    )(
        x0,
        down,
        up,
        bias.reshape(1, -1),
        w,
        mlp_bias.reshape(1, -1),
        mlp_out.reshape(1, -1),
        out_bias.reshape(1, 1),
    )


def on_device(
    cache,
    backing,
    resident,
    promote,
    victim,
    lookups,
    route,
    dcn_down,
    dcn_up,
    dcn_bias,
    mlp_in,
    mlp_bias,
    mlp_out,
    out_bias,
):
    held, slots, block, width = cache.shape
    new_cache, new_backing = promote_blocks(cache, backing, resident, promote, victim)
    codes = routed(lookups, route, lax.axis_size("cache"))
    table = new_cache.reshape(held, slots * block, width)
    x0 = pool(codes, table, lookups.shape[3])
    batches, group = lookups.shape[0], lookups.shape[1]
    here = lax.axis_index("cache")
    devices = lax.axis_size("cache")
    own_dims = x0.shape[1]
    bias = lax.dynamic_slice_in_dim(dcn_bias, here * own_dims, own_dims, 0)
    per = group // devices
    scores = dense_stack(x0, dcn_down, dcn_up, bias, mlp_in, mlp_bias, mlp_out, out_bias)
    return (scores.reshape(batches, 1, per), new_cache, new_backing)


def solution(mesh):
    in_specs = (
        P("cache", None, None, None),
        P("cache", "owner", None, None),
        P("cache", None),
        P("cache", None),
        P("cache", None),
        P(None, "owner", "cache", None),
        P(None, "owner", None),
        P("cache", None),
        P(None, "cache"),
        P(),
        P("cache", None),
        P(),
        P(),
        P(),
    )
    out_specs = (
        P(None, "owner", "cache"),
        P("cache", None, None, None),
        P("cache", "owner", None, None),
    )
    return jax.shard_map(
        on_device, mesh=mesh, in_specs=in_specs, out_specs=out_specs, check_vma=False
    )
```

```python
import jax
import jax.numpy as jnp
from jax import lax
from jax.experimental import pallas as pl
from jax.experimental.pallas import tpu as pltpu
from jax.sharding import PartitionSpec as P


def take_rows(table, wanted):
    return jax.vmap(lambda rows, chosen: rows[chosen])(table, wanted)


def gather_kernel(n, mine_ref, out_ref, near_recv, far_send, far_recv, done_send, done_recv, near_sems, far_sems):
    pair = out_ref.shape[0] // far_send.shape[0]
    lines = n // pair
    part = far_send.shape[0]
    me = lax.axis_index("owner")
    line, side = me // pair, me % pair
    buddy = line * pair + (pair - 1 - side)
    own, other = pl.ds(side * part, part), pl.ds((pair - 1 - side) * part, part)

    def send(src, dst, send_sem, recv_sem, c):
        copy = pltpu.make_async_remote_copy(
            src_ref=src,
            dst_ref=dst,
            send_sem=send_sem,
            recv_sem=recv_sem,
            device_id={"owner": c},
            device_id_type=pl.DeviceIdType.MESH,
        )
        copy.start()
        return copy

    across = [lax.rem(line + o, lines) * pair + side for o in range(1, lines)]
    peers = across + ([buddy] if pair > 1 else [])
    barrier = pltpu.get_barrier_semaphore()
    for c in peers:
        pl.semaphore_signal(barrier, inc=1, device_id={"owner": c}, device_id_type=pl.DeviceIdType.MESH)
    pl.semaphore_wait(barrier, len(peers))

    copies = []
    total = mine_ref[own]
    if pair > 1:
        copy = send(mine_ref.at[other], near_recv, near_sems.at[0, 0], near_sems.at[1, 0], buddy)
        copy.wait_recv()
        total = total + near_recv[...]
        copies.append(copy)
    far_send[...] = total
    fars = [
        send(far_send, far_recv.at[k], far_sems.at[0, k], far_sems.at[1, k], c) for k, c in enumerate(across)
    ]
    for k, copy in enumerate(fars):
        copy.wait_recv()
        total = total + far_recv[k]
    out_ref[own] = total
    if pair > 1:
        done_send[...] = total
        copy = send(done_send, done_recv, near_sems.at[0, 1], near_sems.at[1, 1], buddy)
        copy.wait_recv()
        out_ref[other] = done_recv[...]
        copies.append(copy)
    for copy in copies + fars:
        copy.wait_send()


def everywhere(outgoing):
    n = lax.axis_size("owner")
    held, promoted_count, block, width = outgoing.shape
    blocks = held * promoted_count
    pair = 2 if n % 2 == 0 and blocks % 2 == 0 else 1
    part = (blocks // pair, block, width)
    fars = max(n // pair - 1, 1)
    vmem = pl.BlockSpec(memory_space=pltpu.VMEM)
    got = pl.pallas_call(
        lambda *refs: gather_kernel(n, *refs),
        in_specs=[vmem],
        out_specs=vmem,
        out_shape=jax.ShapeDtypeStruct((blocks, block, width), outgoing.dtype),
        scratch_shapes=[
            pltpu.VMEM(part, outgoing.dtype),
            pltpu.VMEM(part, outgoing.dtype),
            pltpu.VMEM((fars,) + part, outgoing.dtype),
            pltpu.VMEM(part, outgoing.dtype),
            pltpu.VMEM(part, outgoing.dtype),
            pltpu.SemaphoreType.DMA((2, 2)),
            pltpu.SemaphoreType.DMA((2, fars)),
        ],
        compiler_params=pltpu.CompilerParams(collective_id=1, has_side_effects=True),
    )(outgoing.reshape(blocks, block, width))
    return got.reshape(outgoing.shape)


def promote_blocks(cache, backing, resident, promote, victim):
    held, slots, block, width = cache.shape
    own_blocks = backing.shape[1]
    promoted_count = promote.shape[1]
    owner_here = lax.axis_index("owner")
    local_index = promote - owner_here * own_blocks
    owned_here = (local_index >= 0) & (local_index < own_blocks)
    clamped = jnp.clip(local_index, 0, own_blocks - 1)
    fetched = take_rows(backing, clamped)
    outgoing = jnp.where(owned_here[:, :, None, None], fetched, jnp.zeros_like(fetched))
    promoted = everywhere(outgoing)
    evicted = take_rows(cache, victim)
    leaving = take_rows(resident, victim) - owner_here * own_blocks
    slot_numbers = jnp.arange(slots, dtype=jnp.int32)
    block_numbers = jnp.arange(own_blocks, dtype=jnp.int32)
    new_cache = cache
    new_backing = backing
    for column in range(promoted_count):
        slot_hit = victim[:, column][:, None] == slot_numbers[None, :]
        new_cache = jnp.where(slot_hit[:, :, None, None], promoted[:, column][:, None], new_cache)
        block_hit = leaving[:, column][:, None] == block_numbers[None, :]
        new_backing = jnp.where(
            block_hit[:, :, None, None], evicted[:, column][:, None], new_backing
        )
    return new_cache, new_backing


def routed(lookups, route, devices):
    batches, count, held, bag = lookups.shape
    flat = lookups.reshape(batches, count, held * bag)
    halves = jnp.concatenate([flat // 256, flat % 256], axis=-1).astype(jnp.bfloat16)
    pick = (route[:, 0, :, None] == jnp.arange(count, dtype=jnp.int32)).astype(jnp.bfloat16)
    got = jnp.einsum("bpr,brj->bpj", pick, halves, preferred_element_type=jnp.float32)
    upper, lower = jnp.split(got, 2, axis=-1)
    codes = (upper * 256.0 + lower).reshape(batches, devices, count // devices, held * bag)
    return codes.transpose(1, 0, 2, 3).reshape(batches * count, held * bag)


def pool_rows(codes, table_ref, bag):
    held, rows_total, width = table_ref.shape
    step = codes.shape[0]
    lane = lax.broadcasted_iota(jnp.int32, (step, 128), 1).astype(jnp.float32)
    low_lane = lane.astype(jnp.bfloat16)
    high_lane = (lane + 128.0).astype(jnp.bfloat16)
    one = jnp.ones((step, 128), jnp.bfloat16)
    zero = jnp.zeros((step, 128), jnp.bfloat16)
    pooled = []
    for f in range(held):
        parts = [zero] * (rows_total // 128)
        for l in range(bag):
            j = f * bag + l
            spread = jnp.broadcast_to(codes[:, j : j + 1], (step, 128))
            for base in range(0, rows_total, 256):
                near = (spread - float(base)).astype(jnp.bfloat16)
                for half, numbers in enumerate((low_lane, high_lane)):
                    s = base // 128 + half
                    if s < len(parts):
                        parts[s] = parts[s] + jnp.where(near == numbers, one, zero)
        counts = jnp.concatenate(parts, axis=1)
        pooled.append(
            jnp.dot(counts, table_ref[f], preferred_element_type=jnp.float32).astype(jnp.bfloat16)
        )
    return jnp.concatenate(pooled, axis=1)


def dense_kernel(
    n,
    bag,
    codes_ref,
    table_ref,
    down_ref,
    up_ref,
    bias_ref,
    w_ref,
    mlp_bias_ref,
    mlp_out_ref,
    out_bias_ref,
    scores_ref,
    x0_ref,
    low_ref,
    low_send,
    low_recv,
    low_full,
    near_send,
    near_recv,
    far_send,
    far_recv,
    total_ref,
    low_sems,
    full_sems,
    near_sems,
    far_sems,
):
    rows = x0_ref.shape[0] // n
    pair = 2 if n % 2 == 0 else 1
    lines = n // pair
    me = lax.axis_index("cache")
    line, side = me // pair, me % pair

    def at(c):
        return pl.ds(pl.multiple_of(c * rows, rows), rows)

    def to(src, dst, sems, k, c):
        return pltpu.make_async_remote_copy(
            src_ref=src,
            dst_ref=dst,
            send_sem=sems.at[0, k],
            recv_sem=sems.at[1, k],
            device_id={"cache": c},
            device_id_type=pl.DeviceIdType.MESH,
        )

    def send(*args):
        copy = to(*args)
        copy.start()
        return copy

    def await_low(c):
        k = lax.rem(me - c + n, n) - 1
        to(low_full.at[c], low_full.at[c], full_sems, k, c).wait_recv()

    def dense(c):
        x0 = x0_ref[at(c), :]
        gate = jnp.dot(low_full[c], up_ref[...], preferred_element_type=jnp.float32) + bias_ref[...]
        wide = x0.astype(jnp.float32)
        x1 = (wide * gate + wide).astype(jnp.bfloat16)
        return jnp.dot(x1, w_ref[...], preferred_element_type=jnp.float32)

    barrier = pltpu.get_barrier_semaphore()
    for o in range(1, n):
        pl.semaphore_signal(
            barrier, inc=1, device_id={"cache": lax.rem(me + o, n)}, device_id_type=pl.DeviceIdType.MESH
        )
    pl.semaphore_wait(barrier, n - 1)

    @pl.loop(1, n + 1)
    def _(o):
        c = lax.rem(me + o, n)
        x0 = pool_rows(codes_ref[at(c), :], table_ref, bag)
        x0_ref[at(c), :] = x0
        low = jnp.dot(x0, down_ref[...], preferred_element_type=jnp.float32)

        @pl.when(o < n)
        def _():
            low_send[o - 1] = low.astype(jnp.bfloat16)
            send(low_send.at[o - 1], low_recv.at[o - 1], low_sems, o - 1, c)

        @pl.when(o == n)
        def _():
            low_ref[...] = low

    low = low_ref[...]
    copies = [
        to(low_send.at[o - 1], low_recv.at[o - 1], low_sems, o - 1, lax.rem(me + o, n)) for o in range(1, n)
    ]
    for o in range(1, n):
        copies[o - 1].wait_recv()
        low = low + low_recv[o - 1].astype(jnp.float32)
    low_full[me] = low.astype(jnp.bfloat16)
    shares = [
        send(low_full.at[me], low_full.at[me], full_sems, o - 1, lax.rem(me + o, n)) for o in range(1, n)
    ]

    offsets = list(range(1, lines)) + [0]
    nears, fars = [], []

    def first(k):
        c = lax.rem(line + offsets[k], lines) * pair + (pair - 1 - side)
        await_low(c)
        near_send[k] = dense(c).astype(jnp.bfloat16)
        nears.append(send(near_send.at[k], near_recv.at[k], near_sems, k, line * pair + (pair - 1 - side)))

    def second(k):
        c = lax.rem(line + offsets[k], lines) * pair + side
        if offsets[k]:
            await_low(c)
        part = dense(c)
        if pair > 1:
            nears[k].wait_recv()
            part = part + near_recv[k].astype(jnp.float32)
        if offsets[k]:
            far_send[k] = part.astype(jnp.bfloat16)
            fars.append(send(far_send.at[k], far_recv.at[k], far_sems, k, c))
        else:
            total_ref[...] = part

    for k in range(lines + 1):
        if k < lines and pair > 1:
            first(k)
        if k:
            second(k - 1)
    total = total_ref[...]
    for k, copy in enumerate(fars):
        copy.wait_recv()
        total = total + far_recv[k].astype(jnp.float32)
    hidden = jnp.maximum(total + mlp_bias_ref[...], 0.0)
    scores_ref[...] = jnp.sum(hidden * mlp_out_ref[...], axis=1, keepdims=True) + out_bias_ref[...]
    for copy in copies + shares + nears + fars:
        copy.wait_send()


def dense_stack(codes, table, bag, down, up, bias, w, mlp_bias, mlp_out, out_bias):
    n = lax.axis_size("cache")
    rows = codes.shape[0] // n
    rank, hid = down.shape[1], w.shape[1]
    lines = n // 2 if n % 2 == 0 else n
    fars = max(lines - 1, 1)
    vmem = pl.BlockSpec(memory_space=pltpu.VMEM)
    return pl.pallas_call(
        lambda *refs: dense_kernel(n, bag, *refs),
        in_specs=[vmem] * 9,
        out_specs=vmem,
        out_shape=jax.ShapeDtypeStruct((rows, 1), jnp.float32),
        scratch_shapes=[
            pltpu.VMEM((n * rows, down.shape[0]), jnp.bfloat16),
            pltpu.VMEM((rows, rank), jnp.float32),
            pltpu.VMEM((n - 1, rows, rank), jnp.bfloat16),
            pltpu.VMEM((n - 1, rows, rank), jnp.bfloat16),
            pltpu.VMEM((n, rows, rank), jnp.bfloat16),
            pltpu.VMEM((lines, rows, hid), jnp.bfloat16),
            pltpu.VMEM((lines, rows, hid), jnp.bfloat16),
            pltpu.VMEM((fars, rows, hid), jnp.bfloat16),
            pltpu.VMEM((fars, rows, hid), jnp.bfloat16),
            pltpu.VMEM((rows, hid), jnp.float32),
            pltpu.SemaphoreType.DMA((2, n - 1)),
            pltpu.SemaphoreType.DMA((2, n - 1)),
            pltpu.SemaphoreType.DMA((2, lines)),
            pltpu.SemaphoreType.DMA((2, fars)),
        ],
        compiler_params=pltpu.CompilerParams(
            collective_id=0, has_side_effects=True, vmem_limit_bytes=60 * 1024 * 1024
        ),
    )(
        codes,
        table,
        down,
        up,
        bias.reshape(1, -1),
        w,
        mlp_bias.reshape(1, -1),
        mlp_out.reshape(1, -1),
        out_bias.reshape(1, 1),
    )


def on_device(
    cache,
    backing,
    resident,
    promote,
    victim,
    lookups,
    route,
    dcn_down,
    dcn_up,
    dcn_bias,
    mlp_in,
    mlp_bias,
    mlp_out,
    out_bias,
):
    held, slots, block, width = cache.shape
    new_cache, new_backing = promote_blocks(cache, backing, resident, promote, victim)
    codes = routed(lookups, route, lax.axis_size("cache"))
    table = new_cache.reshape(held, slots * block, width)
    batches, group = lookups.shape[0], lookups.shape[1]
    here = lax.axis_index("cache")
    devices = lax.axis_size("cache")
    own_dims = dcn_down.shape[0]
    bias = lax.dynamic_slice_in_dim(dcn_bias, here * own_dims, own_dims, 0)
    per = group // devices
    scores = dense_stack(codes, table, lookups.shape[3], dcn_down, dcn_up, bias, mlp_in, mlp_bias, mlp_out, out_bias)
    return (scores.reshape(batches, 1, per), new_cache, new_backing)


def solution(mesh):
    in_specs = (
        P("cache", None, None, None),
        P("cache", "owner", None, None),
        P("cache", None),
        P("cache", None),
        P("cache", None),
        P(None, "owner", "cache", None),
        P(None, "owner", None),
        P("cache", None),
        P(None, "cache"),
        P(),
        P("cache", None),
        P(),
        P(),
        P(),
    )
    out_specs = (
        P(None, "owner", "cache"),
        P("cache", None, None, None),
        P("cache", "owner", None, None),
    )
    return jax.shard_map(
        on_device, mesh=mesh, in_specs=in_specs, out_specs=out_specs, check_vma=False
    )
```
